256 devices in a mesh: chan: 128 (over z, y, x_lo, core), stn: 2 (over x_hi).
Axes of the slice: x: 4 (x_hi: 2, x_lo: 2; x = x_hi * 2 + x_lo), y: 4, z: 8, core: 2. Of those that a mesh axis runs over, the one named last changes fastest.
Arguments:
- voltages: bfloat16 [2, 1536, 2, 256, 512], P(None, 'chan', None, None, 'stn'), may hold values from -6 to 6
- delay_table: float32 [4096], replicated, may hold values from -8 to 8
- delay_index: int32 [64, 512], P(None, 'stn'), may hold values from 0 to 4094
- delay_fraction: int32 [64, 512], P(None, 'stn'), may hold values from 0 to 65535
- station_subarray: int32 [512], P('stn'), may hold values from 0 to 3
Outputs:
- beams: bfloat16 [2, 64, 2, 256, 1536], P(None, 'stn', None, 'chan')
The draws below stay inside these ranges and needn't reach their ends.
All inputs are finite; a program needn't handle non-finite values.
Results may differ from the reference program's by a relative error of at most 0.0068.
Values may be sent and summed in bfloat16 or wider, within the bound.
A program may use at most 128 MiB of HBM per device.

```python
import math
import jax
import jax.numpy as jnp
from jax import lax

STATIONS = 512
POL = 2
NFFT = 256
TAPS = 12
BEAMS = 64
TABLE = 4096
GROUPS = 4
FRAMES = 1536


def with_ends(drawn, key, smallest, top_value):
    place = [jax.random.randint(jax.random.fold_in(key, axis), (), 0, length) for axis, length in enumerate(drawn.shape)]
    widest = drawn.shape.index(max(drawn.shape))
    beside = place[:widest] + [(place[widest] + 1) % drawn.shape[widest]] + place[widest + 1:]
    return drawn.at[tuple(place)].set(smallest).at[tuple(beside)].set(top_value)


def level_of(key, dims, shards, least, top_value):
    gain, own = 1.0, jax.random.fold_in(key, 6)
    for position, parts in shards:
        steps = jnp.exp(jax.random.uniform(jax.random.fold_in(own, position), (parts,), jnp.float32, least / len(shards), top_value / len(shards)))
        gain = gain * jnp.repeat(steps, dims[position] // parts).reshape([-1 if axis == position else 1 for axis in range(len(dims))])
    return gain


def gaussian(own_key, extent, spread, bound, split=(), kind=jnp.bfloat16):
    entries = jax.random.normal(own_key, extent, jnp.float32) * spread
    if len(split) > 0:
        entries = level_of(own_key, extent, split, -0.22, 0.18) * entries
    return jnp.clip(entries, min=-bound, max=bound).astype(kind)


def setup_inputs(seed: int = 0) -> dict:
    streams_of = jax.random.split(jax.random.key(seed), 6)
    voltages = gaussian(streams_of[0], (POL, FRAMES, 2, NFFT, STATIONS), 1.0, 6.0, ((1, 128), (4, 2)))
    delay_table = jnp.clip(jax.random.uniform(streams_of[1], (TABLE,), jnp.float32, -8.0, 8.0), -8.0, 8.0)
    delay_index = with_ends(jax.random.randint(streams_of[2], (BEAMS, STATIONS), 0, TABLE - 1), jax.random.fold_in(streams_of[2], 1), 0, (TABLE - 1) - 1).astype(jnp.int32)
    delay_fraction = with_ends(jax.random.randint(streams_of[3], (BEAMS, STATIONS), 0, 65536), jax.random.fold_in(streams_of[3], 1), 0, 65535).astype(jnp.int32)
    station_subarray = with_ends(jax.random.randint(streams_of[4], (STATIONS,), 0, GROUPS), jax.random.fold_in(streams_of[4], 1), 0, GROUPS - 1).astype(jnp.int32)
    return {"voltages": voltages, "delay_table": delay_table, "delay_index": delay_index, "delay_fraction": delay_fraction, "station_subarray": station_subarray}


def prototype(tap_count, points):
    length = tap_count * points
    sample_ids = jnp.arange(length, dtype=jnp.float32)
    centred = (sample_ids - (length - 1) / 2.0) / points
    window = 0.5 - 0.5 * jnp.cos(2.0 * math.pi * (sample_ids + 0.5) / length)
    coeffs = jnp.sinc(centred) * window
    coeffs = coeffs * jnp.sqrt(points / jnp.sum(coeffs * coeffs))
    return coeffs.reshape(tap_count, points)

def dft_table(points):
    indices = jnp.arange(points, dtype=jnp.int32)
    product = indices[:, None] * indices[None, :] % points
    angles = 2.0 * math.pi / points * product.astype(jnp.float32)
    cosine = jnp.cos(angles) / math.sqrt(points)
    sine_part = jnp.sin(angles) / math.sqrt(points)
    real_input = jnp.stack([cosine, -sine_part], axis=1)
    imag_input = jnp.stack([sine_part, cosine], axis=1)
    return jnp.stack([real_input, imag_input], axis=0).astype(jnp.bfloat16)

def polyphase(padded, coeffs, frame_count):
    summed = jnp.zeros(padded.shape[:1] + (frame_count,) + padded.shape[2:], jnp.float32)
    for tap_index in range(coeffs.shape[0]):
        summed = summed + coeffs[tap_index][:, None] * padded[:, tap_index:tap_index + frame_count].astype(jnp.float32)
    return summed.astype(jnp.bfloat16)

def steering(delay_table, delay_index, delay_fraction, station_subarray, channel_ids):
    lower_delay = jnp.take(delay_table, delay_index, axis=0)
    upper_delay = jnp.take(delay_table, delay_index + 1, axis=0)
    delays = lower_delay + delay_fraction.astype(jnp.float32) * (1.0 / 65536.0) * (upper_delay - lower_delay)
    beam_ids = jnp.arange(delay_index.shape[0], dtype=jnp.int32)
    member = (station_subarray[None, :] == (beam_ids % GROUPS)[:, None]).astype(jnp.float32) * math.sqrt(GROUPS / STATIONS)
    signed = (channel_ids + NFFT // 2) % NFFT - NFFT // 2
    frequency = signed.astype(jnp.float32) / NFFT
    phases = -2.0 * math.pi * frequency[:, None, None] * delays[None, :, :]
    real_weight = (member * jnp.cos(phases)).astype(jnp.bfloat16)
    imag_weight = (member * jnp.sin(phases)).astype(jnp.bfloat16)
    first_row = jnp.stack([real_weight, -imag_weight], axis=2)
    second_row = jnp.stack([imag_weight, real_weight], axis=2)
    return jnp.stack([first_row, second_row], axis=1)

def reference(voltages, delay_table, delay_index, delay_fraction, station_subarray):
    coeffs = prototype(TAPS, NFFT)
    table_full = dft_table(NFFT).astype(jnp.float32)
    channel_ids = jnp.arange(NFFT, dtype=jnp.int32)
    block_size = min(32, STATIONS)
    block_count = STATIONS // block_size
    zero_frames = jnp.zeros((POL, TAPS - 1, 2, NFFT, block_size), voltages.dtype)

    def add_block(totals, block_index):
        first_row = (block_index * block_size).astype(jnp.int32)
        samples = lax.dynamic_slice_in_dim(voltages, first_row, block_size, 4)
        padded = jnp.concatenate([zero_frames, samples], axis=1)
        filtered = polyphase(padded, coeffs, FRAMES)
        spectra = jnp.einsum('pfiks,ikrc->cprsf', filtered.astype(jnp.float32), table_full, precision=lax.Precision.HIGHEST).astype(jnp.bfloat16)
        weights = steering(delay_table, lax.dynamic_slice_in_dim(delay_index, first_row, block_size, 1), lax.dynamic_slice_in_dim(delay_fraction, first_row, block_size, 1), lax.dynamic_slice_in_dim(station_subarray, first_row, block_size, 0), channel_ids)
        partial_value = lax.dot_general(weights.astype(jnp.float32), spectra.astype(jnp.float32), (((3, 4), (2, 3)), ((0,), (0,))), precision=lax.Precision.HIGHEST)
        return (totals + partial_value, None)
    totals = jnp.zeros((NFFT, 2, BEAMS, POL, FRAMES), jnp.float32)
    totals, unused = lax.scan(add_block, totals, jnp.arange(block_count, dtype=jnp.int32))
    return jnp.transpose(totals, (1, 2, 3, 0, 4)).astype(jnp.bfloat16)
```

```python
import functools
import math

import jax
import jax.numpy as jnp
import numpy as np
from jax import lax
from jax.experimental import pallas as pl
from jax.experimental.pallas import tpu as pltpu
from jax.sharding import Mesh
from jax.sharding import PartitionSpec as P

STATIONS = 512
POL = 2
NFFT = 256
TAPS = 12
GROUPS = 4
CHAN = ("z", "y", "xl", "core")
MESH = pl.DeviceIdType.MESH
F32 = jnp.float32
BF16 = jnp.bfloat16
OUT = 2 * TAPS
KB = 16


def prototype():
    length = TAPS * NFFT
    n = np.arange(length, dtype=np.float64)
    h = np.sinc((n - (length - 1) / 2.0) / NFFT) * (0.5 - 0.5 * np.cos(2.0 * np.pi * (n + 0.5) / length))
    h = h * np.sqrt(NFFT / np.sum(h * h))
    return h.reshape(TAPS, NFFT)


def filter_rows():
    coeffs = prototype()
    rows = np.zeros((2, NFFT // KB, OUT, TAPS, KB), np.float32)
    for out in range(OUT - 1):
        for frame in range(TAPS):
            tap = frame - out + TAPS - 1
            if 0 <= tap < TAPS:
                block = coeffs[tap].reshape(NFFT // KB, KB)
                rows[0, :, out, frame] = block
                rows[1, :, (out + TAPS) % OUT, frame] = block
    return rows.reshape(2, NFFT // KB, OUT, TAPS * KB)


def dft_rows():
    k = np.arange(NFFT)
    angle = (np.float32(2.0 * np.pi / NFFT) * (k[:, None] * k[None, :] % NFFT).astype(np.float32)).astype(np.float32)
    cosine = np.cos(angle).astype(np.float32) / np.float32(math.sqrt(NFFT))
    sine = np.sin(angle).astype(np.float32) / np.float32(math.sqrt(NFFT))
    half = NFFT // 2
    lower = sine[:half].copy()
    lower[0] = cosine[half]
    return np.concatenate([cosine[:half], lower], axis=0)


def beams_kernel(v_ref, rows_ref, dft_ref, table_ref, step_ref, index_ref, fraction_ref, group_ref, out_ref,
                 filt, spec, weight, lists):
    half = NFFT // 2
    stn = v_ref.shape[-1]
    beams = index_ref.shape[0]
    own = beams // GROUPS
    group = group_ref[...]
    index = jnp.zeros((own, stn), jnp.int32)
    fraction = jnp.zeros((own, stn), jnp.int32)
    parts = stn // 128
    for part in range(parts):
        lists[part] = index_ref[:, part * 128:(part + 1) * 128]
        lists[parts + part] = fraction_ref[:, part * 128:(part + 1) * 128]

    def every_fourth(start, g):
        return jnp.concatenate([lists[start + part, pl.ds(g, own, stride=GROUPS), :] for part in range(parts)], axis=1)

    for g in range(GROUPS):
        index = jnp.where(group == g, every_fourth(0, g), index)
        fraction = jnp.where(group == g, every_fourth(parts, g), fraction)
    upper, lower = index // 128, index % 128

    def look(row, found):
        base, rise = found
        here = upper == row
        b_row = jnp.broadcast_to(table_ref[pl.ds(row, 1), :], (own, 128))
        s_row = jnp.broadcast_to(step_ref[pl.ds(row, 1), :], (own, 128))
        b_new, s_new = [], []
        for part in range(stn // 128):
            at = lower[:, part * 128:(part + 1) * 128]
            b_new.append(jnp.take_along_axis(b_row, at, axis=1, mode="promise_in_bounds"))
            s_new.append(jnp.take_along_axis(s_row, at, axis=1, mode="promise_in_bounds"))
        return jnp.where(here, jnp.concatenate(b_new, 1), base), jnp.where(here, jnp.concatenate(s_new, 1), rise)

    zero = jnp.zeros((own, stn), F32)
    base, rise = lax.fori_loop(0, table_ref.shape[0], look, (zero, zero))
    delays = base + fraction.astype(F32) * (1.0 / 65536.0) * rise
    angle = delays * (-2.0 * math.pi / NFFT)
    turn_re, turn_im = jnp.cos(angle), jnp.sin(angle)
    masks = [jnp.where(group == g, math.sqrt(GROUPS / STATIONS), 0.0) for g in range(GROUPS)]

    lane = lax.broadcasted_iota(jnp.int32, (OUT, KB, TAPS * KB), 2) % KB
    row = lax.broadcasted_iota(jnp.int32, (OUT, KB, TAPS * KB), 1)
    diagonal = lane == row

    def filter_block(kb, _):
        lhs = jnp.where(diagonal, rows_ref[kb][:, None, :], 0.0).reshape(OUT * KB, TAPS * KB).astype(BF16)
        at = pl.ds(pl.multiple_of(kb * KB, KB), KB)
        for p in range(POL):
            for i in range(2):
                rhs = v_ref[p, :, i, at, :].reshape(TAPS * KB, stn)
                made = jnp.dot(lhs, rhs, preferred_element_type=F32)
                filt[p * OUT:(p + 1) * OUT, i, at, :] = made.reshape(OUT, KB, stn).astype(BF16)
        return 0

    lax.fori_loop(0, NFFT // KB, filter_block, 0)

    first = lax.broadcasted_iota(jnp.int32, (half, stn), 0) == 0

    def transform(frame, _):
        r = jnp.dot(dft_ref[...], filt[frame, 0], preferred_element_type=F32)
        m = jnp.dot(dft_ref[...], filt[frame, 1], preferred_element_type=F32)
        c_re, s_re, c_im, s_im = r[:half], r[half:], m[:half], m[half:]
        at = pl.ds(pl.multiple_of(frame * half, half), half)
        values = (
            jnp.where(first, c_re, c_re + s_im),
            jnp.where(first, c_im, c_im - s_re),
            jnp.where(first, s_re, c_re - s_im),
            jnp.where(first, s_im, c_im + s_re),
        )
        for which, value in enumerate(values):
            for part in range(stn // 128):
                spec[which, part, at, :] = value[:, part * 128:(part + 1) * 128]
        return 0

    lax.fori_loop(0, POL * OUT, transform, 0)

    rows = POL * OUT
    lanes = lax.broadcasted_iota(jnp.int32, (rows, 128), 1)
    minus_low = jnp.where(lanes < 64, -1.0, 1.0)
    minus_high = -minus_low
    even_chunk = lanes[:OUT] // 32 % 2 == 0
    top = lax.broadcasted_iota(jnp.int32, (OUT, 128), 0) < TAPS

    def take(which, c):
        parts = [spec[which, part, pl.ds(c, rows, stride=half), :] for part in range(stn // 128)]
        return jnp.concatenate(parts, axis=1).astype(BF16)

    def weights(w_re, w_im):
        parts = []
        for value in (w_re, w_im):
            for h in range(2):
                for g in range(GROUPS):
                    parts.append(value[h * own // 2:(h + 1) * own // 2] * masks[g])
        weight[...] = jnp.concatenate(parts, axis=0).astype(BF16)

    def times(lhs):
        return lax.dot_general(lhs, weight[...], (((1,), (1,)), ((), ())), preferred_element_type=F32)

    def positive(re, im):
        return re + minus_low * pltpu.roll(im, 64, 1)

    def negative(re, im):
        return minus_high * re + pltpu.roll(im, 64, 1)

    def both(c, w_re, w_im):
        weights(w_re, w_im)
        made = times(jnp.concatenate([take(which, c) for which in range(4)], axis=0))
        return (positive(made[:rows], made[rows:2 * rows]), negative(made[2 * rows:3 * rows], made[3 * rows:]))

    def by_half(value):
        a, b = value[:OUT], value[OUT:]
        return (jnp.where(even_chunk, a, pltpu.roll(b, 32, 1)), jnp.where(even_chunk, pltpu.roll(a, 96, 1), b))

    def put(owner, even, odd):
        zy, at = owner // 4, owner % 4
        xl, core = at // 2, at % 2
        for h, (e, o) in enumerate(zip(by_half(even), by_half(odd))):
            out_ref[core, h, xl, zy, 0] = jnp.where(top, e, pltpu.roll(o, TAPS, 0)).astype(BF16)
            out_ref[core, h, xl, zy, 1] = jnp.where(top, pltpu.roll(e, TAPS, 0), o).astype(BF16)

    def turned(w):
        return (w[0] * turn_re - w[1] * turn_im, w[0] * turn_im + w[1] * turn_re)

    w = (jnp.ones((own, stn), F32), zero)
    even, _ = both(0, *w)
    w = turned(w)
    odd, carried = both(1, *w)
    w = turned(w)
    put(0, even, odd)

    def pair(d, state):
        w_re, w_im, kept = state
        even, even_minus = both(2 * d, w_re, w_im)
        w = turned((w_re, w_im))
        odd, odd_minus = both(2 * d + 1, *w)
        w = turned(w)
        put(d, even, odd)
        put(half - d, even_minus, kept)
        return w[0], w[1], odd_minus

    w_re, w_im, carried = lax.fori_loop(1, half // 2, pair, (w[0], w[1], carried))
    weights(w_re, w_im)
    made = times(jnp.concatenate([take(2, 0), take(3, 0)], axis=0))
    put(half // 2, negative(made[:rows], made[rows:]), carried)


def beams_call(v, rows, dft, table, step, index, fraction, group, zy):
    stn = v.shape[-1]
    vmem = pl.BlockSpec(memory_space=pltpu.VMEM)
    return pl.pallas_call(
        beams_kernel,
        out_shape=jax.ShapeDtypeStruct((2, 2, 2, zy, 2, OUT, 128), BF16),
        in_specs=[vmem] * 8,
        out_specs=vmem,
        scratch_shapes=[
            pltpu.VMEM((POL * OUT, 2, NFFT, stn), BF16),
            pltpu.VMEM((4, stn // 128, POL * OUT * NFFT // 2, 128), F32),
            pltpu.VMEM((128, stn), BF16),
            pltpu.VMEM((stn // 64, index.shape[0], 128), jnp.int32),
        ],
        compiler_params=pltpu.CompilerParams(vmem_limit_bytes=60 * 1024 * 1024),
        name="partial_beams",
    )(v, rows, dft, table, step, index, fraction, group)


def exchange_kernel(nz, ny, pa, out, r0, m, r1, s2, s_sem, r_sem, local_sem, s1_sem, r1_sem, s2_sem, r2_sem):
    z, y = lax.axis_index("z"), lax.axis_index("y")
    xl, core, xh = lax.axis_index("xl"), lax.axis_index("core"), lax.axis_index("stn")
    zy = z * ny + y
    count = nz * ny

    def row_peer(k):
        place = (xh * 2 + xl + k) % 4
        return (z, y, place % 2, core, place // 2), place

    def column_peer(k):
        place = (zy + k) % count
        return (place // ny, place % ny, xl, core, xh), place

    barrier = pltpu.get_barrier_semaphore()
    pl.semaphore_signal(barrier, inc=1, device_id=(z, y, xl, 1 - core, xh), device_id_type=MESH)
    for k in range(1, 4):
        pl.semaphore_signal(barrier, inc=1, device_id=row_peer(k)[0], device_id_type=MESH)

    def greet(k, _):
        pl.semaphore_signal(barrier, inc=1, device_id=column_peer(k)[0], device_id_type=MESH)
        return 0

    lax.fori_loop(1, count, greet, 0)
    pl.semaphore_wait(barrier, 4 + count - 1)

    first = pltpu.make_async_remote_copy(
        src_ref=pa.at[1 - core], dst_ref=r0, send_sem=s_sem, recv_sem=r_sem,
        device_id=(z, y, xl, 1 - core, xh), device_id_type=MESH)
    first.start()
    first.wait()
    lead = core == 0

    def merge(h, x):
        def body(i, _):
            a0, a1 = pa[core, h, x, i, 0].astype(F32), pa[core, h, x, i, 1].astype(F32)
            b0, b1 = r0[h, x, i, 0].astype(F32), r0[h, x, i, 1].astype(F32)
            m[h, x, i, 0] = jnp.where(lead, a0, b0).astype(BF16)
            m[h, x, i, 1] = (a1 + b1).astype(BF16)
            m[h, x, i, 2] = jnp.where(lead, b0, a0).astype(BF16)
            return 0
        lax.fori_loop(0, count, body, 0)

    here = xh * 2 + xl
    sends = []
    for k in (2, 1, 3, 0):
        device, place = row_peer(k)
        merge(place // 2, place % 2)
        if k == 0:
            copy = pltpu.make_async_copy(m.at[place // 2, place % 2], r1.at[here], local_sem)
        else:
            copy = pltpu.make_async_remote_copy(
                src_ref=m.at[place // 2, place % 2], dst_ref=r1.at[here], send_sem=s1_sem.at[k - 1],
                recv_sem=r1_sem.at[k - 1], device_id=device, device_id_type=MESH)
        copy.start()
        sends.append(copy)
    for copy in sends:
        copy.wait()

    def reduce(i, _):
        t = [[r1[xx, i, g].astype(F32) + r1[2 + xx, i, g].astype(F32) for g in range(3)] for xx in range(2)]
        s2[i, 0] = t[0][0].astype(BF16)
        s2[i, 1] = t[0][1].astype(BF16)
        s2[i, 2] = (t[0][2] + t[1][0]).astype(BF16)
        s2[i, 3] = t[1][1].astype(BF16)
        s2[i, 4] = t[1][2].astype(BF16)
        return 0

    lax.fori_loop(0, count, reduce, 0)

    mine = pltpu.make_async_copy(s2.at[zy], out.at[zy], local_sem)
    mine.start()

    def column(k):
        device, place = column_peer(k)
        return pltpu.make_async_remote_copy(
            src_ref=s2.at[place], dst_ref=out.at[zy], send_sem=s2_sem.at[k], recv_sem=r2_sem.at[k],
            device_id=device, device_id_type=MESH)

    def send(k, _):
        column(k).start()
        return 0

    def finish(k, _):
        column(k).wait()
        return 0

    lax.fori_loop(1, count, send, 0)
    mine.wait()
    lax.fori_loop(1, count, finish, 0)


def exchange_call(pa, nz, ny):
    zy = nz * ny
    vmem = pl.BlockSpec(memory_space=pltpu.VMEM)
    dma = pltpu.SemaphoreType.DMA
    return pl.pallas_call(
        functools.partial(exchange_kernel, nz, ny),
        out_shape=jax.ShapeDtypeStruct((zy, 5, OUT, 128), BF16),
        in_specs=[vmem],
        out_specs=vmem,
        scratch_shapes=[
            pltpu.VMEM((2, 2, zy, 2, OUT, 128), BF16),
            pltpu.VMEM((2, 2, zy, 3, OUT, 128), BF16),
            pltpu.VMEM((4, zy, 3, OUT, 128), BF16),
            pltpu.VMEM((zy, 5, OUT, 128), BF16),
            dma, dma, dma, dma((3,)), dma((3,)), dma((zy,)), dma((zy,)),
        ],
        compiler_params=pltpu.CompilerParams(
            collective_id=0, has_side_effects=True, vmem_limit_bytes=48 * 1024 * 1024),
        name="exchange",
    )(pa)


def finish_kernel(x_ref, out_ref, frames):
    blocks = x_ref.shape[0]
    top = lax.broadcasted_iota(jnp.int32, (OUT, 128), 0) < TAPS
    span = 4 * TAPS

    def gather(b, _):
        segs = [x_ref[b, g].astype(F32) for g in range(4)]
        before = x_ref[jnp.maximum(b - 1, 0), 4].astype(F32)
        segs[0] = segs[0] + jnp.where(b > 0, before, 0.0)
        for j in range(2):
            a, c = segs[2 * j], segs[2 * j + 1]
            at = pl.ds(pl.multiple_of(b * span + j * OUT, 8), OUT)
            frames[0, at, :] = jnp.where(top, a, pltpu.roll(c, TAPS, 0))
            frames[1, at, :] = jnp.where(top, pltpu.roll(a, TAPS, 0), c)
        return 0

    lax.fori_loop(0, blocks, gather, 0)

    def turn(t, _):
        at = pl.ds(pl.multiple_of(t * 128, 128), 128)
        a, c = frames[0, at, :].T, frames[1, at, :].T
        both = jnp.stack([a, c], axis=1).astype(BF16)
        for ro in range(2):
            for p in range(POL):
                for g in range(GROUPS):
                    for jj in range(8):
                        out_ref[ro, 4 * jj + g, p, :, at] = both[ro * 64 + p * 32 + g * 8 + jj]
        return 0

    lax.fori_loop(0, blocks * span // 128, turn, 0)


def finish_call(x):
    blocks = x.shape[0]
    total = blocks * 4 * TAPS
    vmem = pl.BlockSpec(memory_space=pltpu.VMEM)
    return pl.pallas_call(
        finish_kernel,
        out_shape=jax.ShapeDtypeStruct((2, 32, POL, 2, total), BF16),
        in_specs=[vmem],
        out_specs=vmem,
        scratch_shapes=[pltpu.VMEM((2, total, 128), F32)],
        compiler_params=pltpu.CompilerParams(vmem_limit_bytes=32 * 1024 * 1024),
        name="finish",
    )(x)


def shards(voltages, delay_table, delay_index, delay_fraction, station_subarray):
    nz, ny = lax.axis_size("z"), lax.axis_size("y")
    rows = lax.dynamic_index_in_dim(jnp.asarray(filter_rows()), lax.axis_index("core"), 0, keepdims=False)
    dft = jnp.asarray(dft_rows()).astype(BF16)
    step = jnp.concatenate([delay_table[1:], delay_table[-1:]]) - delay_table
    pa = beams_call(voltages, rows, dft, delay_table.reshape(-1, 128), step.reshape(-1, 128), delay_index,
                    delay_fraction, station_subarray.reshape(1, -1), nz * ny)
    return finish_call(exchange_call(pa, nz, ny))


def solution(mesh):
    torus = Mesh(mesh.devices.reshape(8, 4, 2, 2, mesh.shape["stn"]), CHAN + ("stn",))
    placed = (P(None, CHAN, None, None, "stn"), P(), P(None, "stn"), P(None, "stn"), P("stn"))
    return jax.shard_map(
        shards,
        mesh=torus,
        in_specs=placed,
        out_specs=P(None, "stn", None, CHAN, None),
        check_vma=False,
    )
```

```python
import functools
import math

import jax
import jax.numpy as jnp
import numpy as np
from jax import lax
from jax.experimental import pallas as pl
from jax.experimental.pallas import tpu as pltpu
from jax.sharding import Mesh
from jax.sharding import PartitionSpec as P

STATIONS = 512
POL = 2
NFFT = 256
TAPS = 12
GROUPS = 4
CHAN = ("z", "y", "xl", "core")
MESH = pl.DeviceIdType.MESH
F32 = jnp.float32
BF16 = jnp.bfloat16
OUT = 2 * TAPS
CHUNKS = 8
LAG = 3
UNROLL_T = 2
UNROLL_P = 1
KB = 16


def prototype():
    length = TAPS * NFFT
    n = np.arange(length, dtype=np.float64)
    h = np.sinc((n - (length - 1) / 2.0) / NFFT) * (0.5 - 0.5 * np.cos(2.0 * np.pi * (n + 0.5) / length))
    h = h * np.sqrt(NFFT / np.sum(h * h))
    return h.reshape(TAPS, NFFT)


def filter_rows():
    coeffs = prototype()
    rows = np.zeros((NFFT // KB, OUT, TAPS, KB), np.float32)
    for out in range(OUT - 1):
        for frame in range(TAPS):
            tap = frame - out + TAPS - 1
            if 0 <= tap < TAPS:
                rows[:, out, frame] = coeffs[tap].reshape(NFFT // KB, KB)
    return rows.reshape(NFFT // KB, OUT, TAPS * KB)


def dft_rows():
    k = np.arange(NFFT)
    angle = (np.float32(2.0 * np.pi / NFFT) * (k[:, None] * k[None, :] % NFFT).astype(np.float32)).astype(np.float32)
    cosine = np.cos(angle).astype(np.float32) / np.float32(math.sqrt(NFFT))
    sine = np.sin(angle).astype(np.float32) / np.float32(math.sqrt(NFFT))
    half = NFFT // 2
    lower = sine[:half].copy()
    lower[0] = cosine[half]
    return np.concatenate([cosine[:half], lower], axis=0)


def fused_kernel(nz, ny, v_hbm, rows_ref, dft_ref, table_ref, index_ref, fraction_ref, group_ref, out,
                 vbuf, filt, spec, lists, pa, r0, m, r1, s2, v_sem, s0_sem, r0_sem, own_sem, s1_sem, r1_sem, s2_sem,
                 r2_sem, mine_sem):
    half = NFFT // 2
    stn = v_hbm.shape[-1]
    parts = stn // 128
    beams = index_ref.shape[0]
    own = beams // GROUPS
    z, y = lax.axis_index("z"), lax.axis_index("y")
    xl, core, xh = lax.axis_index("xl"), lax.axis_index("core"), lax.axis_index("stn")
    zy = z * ny + y
    count = nz * ny
    steps = half // 2 // CHUNKS
    side = count // CHUNKS // 2

    def row_peer(k):
        place = (xh * 2 + xl + k) % 4
        return (z, y, place % 2, core, place // 2), place

    def column_peer(k):
        place = (zy + k) % count
        return (place // ny, place % ny, xl, core, xh)

    other = (z, y, xl, 1 - core, xh)
    barrier = pltpu.get_barrier_semaphore()
    pl.semaphore_signal(barrier, inc=1, device_id=other, device_id_type=MESH)
    for k in range(1, 4):
        pl.semaphore_signal(barrier, inc=1, device_id=row_peer(k)[0], device_id_type=MESH)

    def greet(k, _):
        pl.semaphore_signal(barrier, inc=1, device_id=column_peer(k), device_id_type=MESH)
        return 0

    lax.fori_loop(1, count, greet, 0)

    def fetch(kb, slot):
        at = pl.ds(pl.multiple_of(kb * KB, KB), KB)
        return pltpu.make_async_copy(v_hbm.at[:, :, :, at, :], vbuf.at[slot], v_sem.at[slot])

    fetch(0, 0).start()

    group = group_ref[...]
    index = jnp.zeros((own, stn), jnp.int32)
    fraction = jnp.zeros((own, stn), jnp.int32)
    for part in range(parts):
        lists[part] = index_ref[:, part * 128:(part + 1) * 128]
        lists[parts + part] = fraction_ref[:, part * 128:(part + 1) * 128]

    def every_fourth(start, g):
        return jnp.concatenate([lists[start + part, pl.ds(g, own, stride=GROUPS), :] for part in range(parts)], axis=1)

    for g in range(GROUPS):
        index = jnp.where(group == g, every_fourth(0, g), index)
        fraction = jnp.where(group == g, every_fourth(parts, g), fraction)
    upper, lower = index // 128, index % 128
    table = table_ref[...]
    table_rows = table.shape[0]
    turned_once = pltpu.roll(table, 127, 1)
    last = lax.broadcasted_iota(jnp.int32, table.shape, 1) == 127
    rise_table = jnp.where(last, pltpu.roll(turned_once, table_rows - 1, 0), turned_once) - table
    base = jnp.zeros((own, stn), F32)
    rise = jnp.zeros((own, stn), F32)
    for row in range(table_rows):
        here = upper == row
        b_row = jnp.broadcast_to(table[row:row + 1], (own, 128))
        s_row = jnp.broadcast_to(rise_table[row:row + 1], (own, 128))
        b_new, s_new = [], []
        for part in range(parts):
            at = lower[:, part * 128:(part + 1) * 128]
            b_new.append(jnp.take_along_axis(b_row, at, axis=1, mode="promise_in_bounds"))
            s_new.append(jnp.take_along_axis(s_row, at, axis=1, mode="promise_in_bounds"))
        base = jnp.where(here, jnp.concatenate(b_new, 1), base)
        rise = jnp.where(here, jnp.concatenate(s_new, 1), rise)
    delays = base + fraction.astype(F32) * (1.0 / 65536.0) * rise
    angle = delays * (-2.0 * math.pi / NFFT)
    turn_re, turn_im = jnp.cos(angle), jnp.sin(angle)
    masks = [jnp.where(group == g, math.sqrt(GROUPS / STATIONS), 0.0) for g in range(GROUPS)]

    lane = lax.broadcasted_iota(jnp.int32, (OUT, KB, TAPS * KB), 2) % KB
    sample = lax.broadcasted_iota(jnp.int32, (OUT, KB, TAPS * KB), 1)
    diagonal = lane == sample
    blocks = NFFT // KB

    def filter_block(kb, _):
        slot = kb % 2
        fetch(kb, slot).wait()

        @pl.when(kb + 1 < blocks)
        def _():
            fetch(kb + 1, 1 - slot).start()

        taps = rows_ref[kb]
        taps = jnp.where(core == 0, taps, pltpu.roll(taps, TAPS, 0))
        lhs = jnp.where(diagonal, taps[:, None, :], 0.0).reshape(OUT * KB, TAPS * KB).astype(BF16)
        at = pl.ds(pl.multiple_of(kb * KB, KB), KB)
        for p in range(POL):
            for i in range(2):
                rhs = vbuf[slot, p, :, i].reshape(TAPS * KB, stn)
                made = jnp.dot(lhs, rhs, preferred_element_type=F32)
                filt[p * OUT:(p + 1) * OUT, i, at, :] = made.reshape(OUT, KB, stn).astype(BF16)
        return 0

    lax.fori_loop(0, blocks, filter_block, 0)

    first = lax.broadcasted_iota(jnp.int32, (half, stn), 0) == 0

    def transform(frame, _):
        r = jnp.dot(dft_ref[...], filt[frame, 0], preferred_element_type=F32)
        i = jnp.dot(dft_ref[...], filt[frame, 1], preferred_element_type=F32)
        c_re, s_re, c_im, s_im = r[:half], r[half:], i[:half], i[half:]
        at = pl.ds(pl.multiple_of(frame * 8, 8), 8)
        values = (
            jnp.where(first, c_re, c_re + s_im),
            jnp.where(first, c_im, c_im - s_re),
            jnp.where(first, s_re, c_re - s_im),
            jnp.where(first, s_im, c_im + s_re),
        )
        for which, value in enumerate(values):
            for part in range(parts):
                spec[which, part, :, at, :] = value[:, part * 128:(part + 1) * 128].reshape(half // 8, 8, 128)
        return 0

    lax.fori_loop(0, POL * OUT, transform, 0, unroll=UNROLL_T)

    rows = POL * OUT
    lanes = lax.broadcasted_iota(jnp.int32, (rows, 128), 1)
    minus_low = jnp.where(lanes < 64, -1.0, 1.0)
    minus_high = -minus_low
    even_chunk = lanes[:OUT] // 32 % 2 == 0
    top = lax.broadcasted_iota(jnp.int32, (OUT, 128), 0) < TAPS

    def take(which, c):
        tile, line = c // 8 % (half // 8), c % 8
        found = [spec[which, part, tile, pl.ds(line, rows, stride=8), :] for part in range(parts)]
        return jnp.concatenate(found, axis=1).astype(BF16)

    def weights(w_re, w_im):
        made = []
        for value in (w_re, w_im):
            for h in range(2):
                for g in range(GROUPS):
                    made.append(value[h * own // 2:(h + 1) * own // 2] * masks[g])
        return jnp.concatenate(made, axis=0).astype(BF16)

    def times(lhs, w):
        return lax.dot_general(lhs, w, (((1,), (1,)), ((), ())), preferred_element_type=F32)

    def positive(re, im):
        return re + minus_low * pltpu.roll(im, 64, 1)

    def negative(re, im):
        return minus_high * re + pltpu.roll(im, 64, 1)

    def both(c, w):
        made = times(jnp.concatenate([take(which, c) for which in range(4)], axis=0), weights(*w))
        return positive(made[:rows], made[rows:2 * rows]), negative(made[2 * rows:3 * rows], made[3 * rows:])

    def by_half(value):
        a, b = value[:OUT], value[OUT:]
        return jnp.where(even_chunk, a, pltpu.roll(b, 32, 1)), jnp.where(even_chunk, pltpu.roll(a, 96, 1), b)

    def put(owner, q, slot, even, odd):
        at = owner % 4
        to_xl, to_core = at // 2, at % 2
        for h, (e, o) in enumerate(zip(by_half(even), by_half(odd))):
            pa[to_core, q, h, to_xl, slot, 0] = jnp.where(top, e, pltpu.roll(o, TAPS, 0)).astype(BF16)
            pa[to_core, q, h, to_xl, slot, 1] = jnp.where(top, pltpu.roll(e, TAPS, 0), o).astype(BF16)

    def turned(w):
        return (w[0] * turn_re - w[1] * turn_im, w[0] * turn_im + w[1] * turn_re)

    def chunk(t):
        return (t + z) % CHUNKS

    def make(t):
        q = chunk(t)
        begin = q * steps
        here = angle * (2 * begin).astype(F32)
        w = (jnp.cos(here), jnp.sin(here))
        made = times(jnp.concatenate([take(which, 2 * begin) for which in range(2)], axis=0), weights(*w))
        even = positive(made[:rows], made[rows:])
        w = turned(w)

        def pair(i, state):
            w_re, w_im, even = state
            e = begin + i
            odd, odd_minus = both(2 * e + 1, (w_re, w_im))
            w = turned((w_re, w_im))
            later, even_minus = both(2 * e + 2, w)
            w = turned(w)
            put(e, t, i // 4, even, odd)
            put(half - 1 - e, t, side + i // 4, even_minus, odd_minus)
            return w[0], w[1], later

        lax.fori_loop(0, steps, pair, (w[0], w[1], even), unroll=UNROLL_P)

    def place(t, slot):
        at = chunk(t) * side + slot % side
        return jnp.where(slot < side, at, count - 1 - at)

    lead = core == 0

    def pair_copy(t):
        return pltpu.make_async_remote_copy(
            src_ref=pa.at[1 - core, t], dst_ref=r0.at[t], send_sem=s0_sem.at[t], recv_sem=r0_sem.at[t],
            device_id=other, device_id_type=MESH)

    def row_copy(t, k):
        device, to = row_peer(k)
        return pltpu.make_async_remote_copy(
            src_ref=m.at[t, to // 2, to % 2], dst_ref=r1.at[t, xh * 2 + xl], send_sem=s1_sem.at[t, k - 1],
            recv_sem=r1_sem.at[t, k - 1], device_id=device, device_id_type=MESH)

    def own_copy(t):
        return pltpu.make_async_copy(m.at[t, xh, xl], r1.at[t, xh * 2 + xl], own_sem.at[t])

    def column_copy(t, slot, k):
        return pltpu.make_async_remote_copy(
            src_ref=s2.at[t, slot], dst_ref=out.at[zy], send_sem=s2_sem.at[k], recv_sem=r2_sem.at[k],
            device_id=column_peer(k), device_id_type=MESH)

    def merge(t):
        for h in range(2):
            for x in range(2):
                def body(i, _):
                    a0, a1 = pa[core, t, h, x, i, 0].astype(F32), pa[core, t, h, x, i, 1].astype(F32)
                    b0, b1 = r0[t, h, x, i, 0].astype(F32), r0[t, h, x, i, 1].astype(F32)
                    m[t, h, x, i, 0] = jnp.where(lead, a0, b0).astype(BF16)
                    m[t, h, x, i, 1] = (a1 + b1).astype(BF16)
                    m[t, h, x, i, 2] = jnp.where(lead, b0, a0).astype(BF16)
                    return 0
                lax.fori_loop(0, 2 * side, body, 0, unroll=True)

    def reduce(t):
        def body(i, _):
            s = [[r1[t, x, i, g].astype(F32) + r1[t, 2 + x, i, g].astype(F32) for g in range(3)] for x in range(2)]
            s2[t, i, 0] = s[0][0].astype(BF16)
            s2[t, i, 1] = s[0][1].astype(BF16)
            s2[t, i, 2] = (s[0][2] + s[1][0]).astype(BF16)
            s2[t, i, 3] = s[1][1].astype(BF16)
            s2[t, i, 4] = s[1][2].astype(BF16)
            return 0
        lax.fori_loop(0, 2 * side, body, 0, unroll=True)

    pl.semaphore_wait(barrier, 4 + count - 1)

    def run(t, _):
        @pl.when(t < CHUNKS)
        def _():
            make(t)
            pair_copy(t).start()

        @pl.when(jnp.logical_and(t >= 1, t <= CHUNKS))
        def _():
            pair_copy(t - 1).wait()
            merge(t - 1)
            for k in (2, 1, 3):
                row_copy(t - 1, k).start()
            own_copy(t - 1).start()

        @pl.when(t >= LAG)
        def _():
            for k in (2, 1, 3):
                row_copy(t - LAG, k).wait()
            own_copy(t - LAG).wait()
            reduce(t - LAG)

            def send(slot, _):
                k = (place(t - LAG, slot) + count - zy) % count

                @pl.when(k != 0)
                def _():
                    column_copy(t - LAG, slot, k).start()

                @pl.when(k == 0)
                def _():
                    mine = pltpu.make_async_copy(s2.at[t - LAG, slot], out.at[zy], mine_sem)
                    mine.start()
                    mine.wait()
                return 0

            lax.fori_loop(0, 2 * side, send, 0)

        return 0

    lax.fori_loop(0, CHUNKS + LAG, run, 0)

    def finish(k, _):
        column_copy(0, 0, k).wait()
        return 0

    lax.fori_loop(1, count, finish, 0)


def fused_call(v, rows, dft, table, index, fraction, group, nz, ny):
    stn = v.shape[-1]
    zy = nz * ny
    slots = zy // CHUNKS
    vmem = pl.BlockSpec(memory_space=pltpu.VMEM)
    dma = pltpu.SemaphoreType.DMA
    return pl.pallas_call(
        functools.partial(fused_kernel, nz, ny),
        out_shape=jax.ShapeDtypeStruct((zy, 5, OUT, 128), BF16),
        in_specs=[pl.BlockSpec(memory_space=pl.ANY)] + [vmem] * 6,
        out_specs=vmem,
        scratch_shapes=[
            pltpu.VMEM((2, POL, TAPS, 2, KB, stn), BF16),
            pltpu.VMEM((POL * OUT, 2, NFFT, stn), BF16),
            pltpu.VMEM((4, stn // 128, NFFT // 16, POL * OUT * 8, 128), F32),
            pltpu.VMEM((stn // 64, index.shape[0], 128), jnp.int32),
            pltpu.VMEM((2, CHUNKS, 2, 2, slots, 2, OUT, 128), BF16),
            pltpu.VMEM((CHUNKS, 2, 2, slots, 2, OUT, 128), BF16),
            pltpu.VMEM((CHUNKS, 2, 2, slots, 3, OUT, 128), BF16),
            pltpu.VMEM((CHUNKS, 4, slots, 3, OUT, 128), BF16),
            pltpu.VMEM((CHUNKS, slots, 5, OUT, 128), BF16),
            dma((2,)), dma((CHUNKS,)), dma((CHUNKS,)), dma((CHUNKS,)), dma((CHUNKS, 3)), dma((CHUNKS, 3)),
            dma((zy,)), dma((zy,)), dma,
        ],
        compiler_params=pltpu.CompilerParams(
            collective_id=0, has_side_effects=True, vmem_limit_bytes=62 * 1024 * 1024),
        name="beams",
    )(v, rows, dft, table, index, fraction, group)


def finish_kernel(x_ref, out_ref, frames):
    blocks = x_ref.shape[0]
    top = lax.broadcasted_iota(jnp.int32, (OUT, 128), 0) < TAPS
    span = 4 * TAPS

    def gather(b, _):
        segs = [x_ref[b, g].astype(F32) for g in range(4)]
        before = x_ref[jnp.maximum(b - 1, 0), 4].astype(F32)
        segs[0] = segs[0] + jnp.where(b > 0, before, 0.0)
        for j in range(2):
            a, c = segs[2 * j], segs[2 * j + 1]
            at = pl.ds(pl.multiple_of(b * span + j * OUT, 8), OUT)
            frames[0, at, :] = jnp.where(top, a, pltpu.roll(c, TAPS, 0))
            frames[1, at, :] = jnp.where(top, pltpu.roll(a, TAPS, 0), c)
        return 0

    lax.fori_loop(0, blocks, gather, 0)

    def turn(t, _):
        at = pl.ds(pl.multiple_of(t * 128, 128), 128)
        a, c = frames[0, at, :].T, frames[1, at, :].T
        both = jnp.stack([a, c], axis=1).astype(BF16)
        for ro in range(2):
            for p in range(POL):
                for g in range(GROUPS):
                    for jj in range(8):
                        out_ref[ro, 4 * jj + g, p, :, at] = both[ro * 64 + p * 32 + g * 8 + jj]
        return 0

    lax.fori_loop(0, blocks * span // 128, turn, 0)


def finish_call(x):
    blocks = x.shape[0]
    total = blocks * 4 * TAPS
    vmem = pl.BlockSpec(memory_space=pltpu.VMEM)
    return pl.pallas_call(
        finish_kernel,
        out_shape=jax.ShapeDtypeStruct((2, 32, POL, 2, total), BF16),
        in_specs=[vmem],
        out_specs=vmem,
        scratch_shapes=[pltpu.VMEM((2, total, 128), F32)],
        compiler_params=pltpu.CompilerParams(vmem_limit_bytes=32 * 1024 * 1024),
        name="finish",
    )(x)


def shards(voltages, delay_table, delay_index, delay_fraction, station_subarray):
    nz, ny = lax.axis_size("z"), lax.axis_size("y")
    rows = jnp.asarray(filter_rows())
    dft = jnp.asarray(dft_rows()).astype(BF16)
    found = fused_call(voltages, rows, dft, delay_table.reshape(-1, 128), delay_index, delay_fraction,
                       station_subarray.reshape(1, -1), nz, ny)
    return finish_call(found)


def solution(mesh):
    torus = Mesh(mesh.devices.reshape(8, 4, 2, 2, mesh.shape["stn"]), CHAN + ("stn",))
    placed = (P(None, CHAN, None, None, "stn"), P(), P(None, "stn"), P(None, "stn"), P("stn"))
    return jax.shard_map(
        shards,
        mesh=torus,
        in_specs=placed,
        out_specs=P(None, "stn", None, CHAN, None),
        check_vma=False,
    )
```

```python
import functools
import math

import jax
import jax.numpy as jnp
import numpy as np
from jax import lax
from jax.experimental import pallas as pl
from jax.experimental.pallas import tpu as pltpu
from jax.sharding import Mesh
from jax.sharding import PartitionSpec as P

STATIONS = 512
POL = 2
NFFT = 256
TAPS = 12
GROUPS = 4
CHAN = ("z", "y", "xl", "core")
MESH = pl.DeviceIdType.MESH
F32 = jnp.float32
BF16 = jnp.bfloat16
OUT = 2 * TAPS
LAG = 4
KB = 16


def prototype():
    length = TAPS * NFFT
    n = np.arange(length, dtype=np.float64)
    h = np.sinc((n - (length - 1) / 2.0) / NFFT) * (0.5 - 0.5 * np.cos(2.0 * np.pi * (n + 0.5) / length))
    h = h * np.sqrt(NFFT / np.sum(h * h))
    return h.reshape(TAPS, NFFT)


def filter_rows():
    coeffs = prototype()
    rows = np.zeros((NFFT // KB, OUT, TAPS, KB), np.float32)
    for out in range(OUT - 1):
        for frame in range(TAPS):
            tap = frame - out + TAPS - 1
            if 0 <= tap < TAPS:
                rows[:, out, frame] = coeffs[tap].reshape(NFFT // KB, KB)
    return rows.reshape(NFFT // KB, OUT, TAPS * KB)


def dft_rows():
    k = np.arange(NFFT)
    angle = (np.float32(2.0 * np.pi / NFFT) * (k[:, None] * k[None, :] % NFFT).astype(np.float32)).astype(np.float32)
    cosine = np.cos(angle).astype(np.float32) / np.float32(math.sqrt(NFFT))
    sine = np.sin(angle).astype(np.float32) / np.float32(math.sqrt(NFFT))
    half = NFFT // 2
    lower = sine[:half].copy()
    lower[0] = cosine[half]
    return np.concatenate([cosine[:half], lower], axis=0)


def fused_kernel(nz, ny, v_hbm, rows_ref, dft_ref, table_ref, index_ref, fraction_ref, group_ref, out,
                 vbuf, filt, spec, lists, pa, r0, m, r1, s2, v_sem, s0_sem, r0_sem, own_sem, s1_sem, r1_sem, s2_sem,
                 r2_sem, mine_sem):
    half = NFFT // 2
    stn = v_hbm.shape[-1]
    parts = stn // 128
    beams = index_ref.shape[0]
    own = beams // GROUPS
    z, y = lax.axis_index("z"), lax.axis_index("y")
    xl, core, xh = lax.axis_index("xl"), lax.axis_index("core"), lax.axis_index("stn")
    zy = z * ny + y
    count = nz * ny
    chunks = count // 2
    steps = half // 2 // chunks

    def row_peer(k):
        place = lax.rem(xh * 2 + xl + k, 4)
        return (z, y, lax.rem(place, 2), core, lax.div(place, 2)), place

    def column_peer(k):
        place = lax.rem(zy + k, count)
        return (lax.div(place, ny), lax.rem(place, ny), xl, core, xh)

    other = (z, y, xl, 1 - core, xh)
    barrier = pltpu.get_barrier_semaphore()
    pl.semaphore_signal(barrier, inc=1, device_id=other, device_id_type=MESH)
    for k in range(1, 4):
        pl.semaphore_signal(barrier, inc=1, device_id=row_peer(k)[0], device_id_type=MESH)

    def greet(k, _):
        pl.semaphore_signal(barrier, inc=1, device_id=column_peer(k), device_id_type=MESH)
        return 0

    lax.fori_loop(1, count, greet, 0)

    def fetch(kb, slot):
        at = pl.ds(pl.multiple_of(kb * KB, KB), KB)
        return pltpu.make_async_copy(v_hbm.at[:, :, :, at, :], vbuf.at[slot], v_sem.at[slot])

    fetch(0, 0).start()

    group = group_ref[...]
    index = jnp.zeros((own, stn), jnp.int32)
    fraction = jnp.zeros((own, stn), jnp.int32)
    for part in range(parts):
        lists[part] = index_ref[:, part * 128:(part + 1) * 128]
        lists[parts + part] = fraction_ref[:, part * 128:(part + 1) * 128]

    def every_fourth(start, g):
        return jnp.concatenate([lists[start + part, pl.ds(g, own, stride=GROUPS), :] for part in range(parts)], axis=1)

    for g in range(GROUPS):
        index = jnp.where(group == g, every_fourth(0, g), index)
        fraction = jnp.where(group == g, every_fourth(parts, g), fraction)
    upper, lower = lax.div(index, 128), lax.rem(index, 128)
    table = table_ref[...]
    table_rows = table.shape[0]
    turned_once = pltpu.roll(table, 127, 1)
    last = lax.broadcasted_iota(jnp.int32, table.shape, 1) == 127
    rise_table = jnp.where(last, pltpu.roll(turned_once, table_rows - 1, 0), turned_once) - table
    base = jnp.zeros((own, stn), F32)
    rise = jnp.zeros((own, stn), F32)
    for row in range(table_rows):
        here = upper == row
        b_row = jnp.broadcast_to(table[row:row + 1], (own, 128))
        s_row = jnp.broadcast_to(rise_table[row:row + 1], (own, 128))
        b_new, s_new = [], []
        for part in range(parts):
            at = lower[:, part * 128:(part + 1) * 128]
            b_new.append(jnp.take_along_axis(b_row, at, axis=1, mode="promise_in_bounds"))
            s_new.append(jnp.take_along_axis(s_row, at, axis=1, mode="promise_in_bounds"))
        base = jnp.where(here, jnp.concatenate(b_new, 1), base)
        rise = jnp.where(here, jnp.concatenate(s_new, 1), rise)
    delays = base + fraction.astype(F32) * (1.0 / 65536.0) * rise
    angle = delays * (-2.0 * math.pi / NFFT)
    turn_re, turn_im = jnp.cos(angle), jnp.sin(angle)
    masks = [jnp.where(group == g, math.sqrt(GROUPS / STATIONS), 0.0) for g in range(GROUPS)]

    lane = lax.broadcasted_iota(jnp.int32, (OUT, KB, TAPS * KB), 2) % KB
    sample = lax.broadcasted_iota(jnp.int32, (OUT, KB, TAPS * KB), 1)
    diagonal = lane == sample
    blocks = NFFT // KB

    def filter_block(kb, _):
        slot = lax.rem(kb, 2)
        fetch(kb, slot).wait()

        @pl.when(kb + 1 < blocks)
        def _():
            fetch(kb + 1, 1 - slot).start()

        taps = rows_ref[kb]
        taps = jnp.where(core == 0, taps, pltpu.roll(taps, TAPS, 0))
        lhs = jnp.where(diagonal, taps[:, None, :], 0.0).reshape(OUT * KB, TAPS * KB).astype(BF16)
        at = pl.ds(pl.multiple_of(kb * KB, KB), KB)
        for p in range(POL):
            for i in range(2):
                rhs = vbuf[slot, p, :, i].reshape(TAPS * KB, stn)
                made = jnp.dot(lhs, rhs, preferred_element_type=F32)
                filt[p * OUT:(p + 1) * OUT, i, at, :] = made.reshape(OUT, KB, stn).astype(BF16)
        return 0

    lax.fori_loop(0, blocks, filter_block, 0, unroll=2)

    first = lax.broadcasted_iota(jnp.int32, (half, stn), 0) == 0

    def transform(frame, _):
        r = jnp.dot(dft_ref[...], filt[frame, 0], preferred_element_type=F32)
        i = jnp.dot(dft_ref[...], filt[frame, 1], preferred_element_type=F32)
        c_re, s_re, c_im, s_im = r[:half], r[half:], i[:half], i[half:]
        at = pl.ds(pl.multiple_of(frame * 8, 8), 8)
        values = (
            jnp.where(first, c_re, c_re + s_im),
            jnp.where(first, c_im, c_im - s_re),
            jnp.where(first, s_re, c_re - s_im),
            jnp.where(first, s_im, c_im + s_re),
        )
        for which, value in enumerate(values):
            for part in range(parts):
                spec[which, part, :, at, :] = value[:, part * 128:(part + 1) * 128].reshape(half // 8, 8, 128)
        return 0

    lax.fori_loop(0, POL * OUT, transform, 0, unroll=2)

    rows = POL * OUT
    lanes = lax.broadcasted_iota(jnp.int32, (rows, 128), 1)
    minus_low = jnp.where(lanes < 64, -1.0, 1.0)
    minus_high = -minus_low
    even_chunk = lanes[:OUT] // 32 % 2 == 0
    top = lax.broadcasted_iota(jnp.int32, (OUT, 128), 0) < TAPS

    def take(which, c):
        tile, line = lax.rem(lax.div(c, 8), half // 8), lax.rem(c, 8)
        found = [spec[which, part, tile, pl.ds(line, rows, stride=8), :] for part in range(parts)]
        return jnp.concatenate(found, axis=1).astype(BF16)

    def weights(w_re, w_im):
        made = []
        for value in (w_re, w_im):
            for h in range(2):
                for g in range(GROUPS):
                    made.append(value[h * own // 2:(h + 1) * own // 2] * masks[g])
        return jnp.concatenate(made, axis=0).astype(BF16)

    def times(lhs, w):
        return lax.dot_general(lhs, w, (((1,), (1,)), ((), ())), preferred_element_type=F32)

    def positive(re, im):
        return re + minus_low * pltpu.roll(im, 64, 1)

    def negative(re, im):
        return minus_high * re + pltpu.roll(im, 64, 1)

    def beamed(c, w, signs):
        made = times(jnp.concatenate([take(2 * sign + i, c) for sign in signs for i in range(2)], axis=0), weights(*w))
        found = []
        for n, sign in enumerate(signs):
            re, im = made[2 * n * rows:(2 * n + 1) * rows], made[(2 * n + 1) * rows:(2 * n + 2) * rows]
            found.append(negative(re, im) if sign else positive(re, im))
        return found

    def by_half(value):
        a, b = value[:OUT], value[OUT:]
        return jnp.where(even_chunk, a, pltpu.roll(b, 32, 1)), jnp.where(even_chunk, pltpu.roll(a, 96, 1), b)

    def put(t, at, slot, even, odd):
        for h, (e, o) in enumerate(zip(by_half(even), by_half(odd))):
            pa[at % 2, t, h, at // 2, slot, 0] = jnp.where(top, e, pltpu.roll(o, TAPS, 0)).astype(BF16)
            pa[at % 2, t, h, at // 2, slot, 1] = jnp.where(top, pltpu.roll(e, TAPS, 0), o).astype(BF16)

    def turned(w):
        return (w[0] * turn_re - w[1] * turn_im, w[0] * turn_im + w[1] * turn_re)

    def chunk(t):
        return lax.rem(t + z, chunks // ny) * ny + lax.rem(lax.div(t, chunks // ny) + y, ny)

    def make(t):
        begin = chunk(t) * (2 * steps)
        here = angle * begin.astype(F32)
        w = (jnp.cos(here), jnp.sin(here))
        even, = beamed(begin, w, (0,))
        for e in range(steps):
            w = turned(w)
            odd, odd_minus = beamed(begin + 2 * e + 1, w, (0, 1))
            put(t, e, 0, even, odd)
            w = turned(w)
            if e < steps - 1:
                even, even_minus = beamed(begin + 2 * e + 2, w, (0, 1))
            else:
                even_minus, = beamed(begin + 2 * e + 2, w, (1,))
            put(t, steps - 1 - e, 1, even_minus, odd_minus)

    lead = core == 0

    def pair_copy(t):
        return pltpu.make_async_remote_copy(
            src_ref=pa.at[1 - core, t], dst_ref=r0.at[t], send_sem=s0_sem.at[t], recv_sem=r0_sem.at[t],
            device_id=other, device_id_type=MESH)

    def row_copy(t, k):
        device, to = row_peer(k)
        return pltpu.make_async_remote_copy(
            src_ref=m.at[t, to // 2, to % 2], dst_ref=r1.at[t, xh * 2 + xl], send_sem=s1_sem.at[t, k - 1],
            recv_sem=r1_sem.at[t, k - 1], device_id=device, device_id_type=MESH)

    def own_copy(t):
        return pltpu.make_async_copy(m.at[t, xh, xl], r1.at[t, xh * 2 + xl], own_sem.at[t])

    def column_copy(t, slot, k):
        return pltpu.make_async_remote_copy(
            src_ref=s2.at[t, slot], dst_ref=out.at[zy], send_sem=s2_sem.at[k], recv_sem=r2_sem.at[k],
            device_id=column_peer(k), device_id_type=MESH)

    def merge(t):
        for h in range(2):
            for x in range(2):
                def body(i, _):
                    a0, a1 = pa[core, t, h, x, i, 0].astype(F32), pa[core, t, h, x, i, 1].astype(F32)
                    b0, b1 = r0[t, h, x, i, 0].astype(F32), r0[t, h, x, i, 1].astype(F32)
                    m[t, h, x, i, 0] = jnp.where(lead, a0, b0).astype(BF16)
                    m[t, h, x, i, 1] = (a1 + b1).astype(BF16)
                    m[t, h, x, i, 2] = jnp.where(lead, b0, a0).astype(BF16)
                    return 0
                lax.fori_loop(0, 2, body, 0, unroll=True)

    def reduce(t):
        def body(i, _):
            s = [[r1[t, x, i, g].astype(F32) + r1[t, 2 + x, i, g].astype(F32) for g in range(3)] for x in range(2)]
            s2[t, i, 0] = s[0][0].astype(BF16)
            s2[t, i, 1] = s[0][1].astype(BF16)
            s2[t, i, 2] = (s[0][2] + s[1][0]).astype(BF16)
            s2[t, i, 3] = s[1][1].astype(BF16)
            s2[t, i, 4] = s[1][2].astype(BF16)
            return 0
        lax.fori_loop(0, 2, body, 0, unroll=True)

    pl.semaphore_wait(barrier, 4 + count - 1)

    def run(t, _):
        @pl.when(t < chunks)
        def _():
            make(t)
            pair_copy(t).start()

        @pl.when(jnp.logical_and(t >= 1, t <= chunks))
        def _():
            pair_copy(t - 1).wait()
            merge(t - 1)
            for k in (2, 1, 3):
                row_copy(t - 1, k).start()
            own_copy(t - 1).start()

        @pl.when(t >= LAG)
        def _():
            for k in (2, 1, 3):
                row_copy(t - LAG, k).wait()
            own_copy(t - LAG).wait()
            reduce(t - LAG)

            for slot in range(2):
                to = chunk(t - LAG)
                k = lax.rem((count - 1 - to if slot else to) + count - zy, count)

                @pl.when(k != 0)
                def _(slot=slot, k=k):
                    column_copy(t - LAG, slot, k).start()

                @pl.when(k == 0)
                def _(slot=slot):
                    mine = pltpu.make_async_copy(s2.at[t - LAG, slot], out.at[zy], mine_sem)
                    mine.start()
                    mine.wait()

        return 0

    lax.fori_loop(0, chunks + LAG, run, 0)

    def finish(k, _):
        column_copy(0, 0, k).wait()
        return 0

    lax.fori_loop(1, count, finish, 0)


def fused_call(v, rows, dft, table, index, fraction, group, nz, ny):
    stn = v.shape[-1]
    zy = nz * ny
    chunks = zy // 2
    slots = 2
    vmem = pl.BlockSpec(memory_space=pltpu.VMEM)
    dma = pltpu.SemaphoreType.DMA
    return pl.pallas_call(
        functools.partial(fused_kernel, nz, ny),
        out_shape=jax.ShapeDtypeStruct((zy, 5, OUT, 128), BF16),
        in_specs=[pl.BlockSpec(memory_space=pl.ANY)] + [vmem] * 6,
        out_specs=vmem,
        scratch_shapes=[
            pltpu.VMEM((2, POL, TAPS, 2, KB, stn), BF16),
            pltpu.VMEM((POL * OUT, 2, NFFT, stn), BF16),
            pltpu.VMEM((4, stn // 128, NFFT // 16, POL * OUT * 8, 128), F32),
            pltpu.VMEM((stn // 64, index.shape[0], 128), jnp.int32),
            pltpu.VMEM((2, chunks, 2, 2, slots, 2, OUT, 128), BF16),
            pltpu.VMEM((chunks, 2, 2, slots, 2, OUT, 128), BF16),
            pltpu.VMEM((chunks, 2, 2, slots, 3, OUT, 128), BF16),
            pltpu.VMEM((chunks, 4, slots, 3, OUT, 128), BF16),
            pltpu.VMEM((chunks, slots, 5, OUT, 128), BF16),
            dma((2,)), dma((chunks,)), dma((chunks,)), dma((chunks,)), dma((chunks, 3)), dma((chunks, 3)),
            dma((zy,)), dma((zy,)), dma,
        ],
        compiler_params=pltpu.CompilerParams(
            collective_id=0, has_side_effects=True, vmem_limit_bytes=62 * 1024 * 1024),
        name="beams",
    )(v, rows, dft, table, index, fraction, group)


def finish_kernel(x_ref, out_ref, frames):
    blocks = x_ref.shape[0]
    top = lax.broadcasted_iota(jnp.int32, (OUT, 128), 0) < TAPS
    span = 4 * TAPS

    def gather(b, _):
        segs = [x_ref[b, g].astype(F32) for g in range(4)]
        before = x_ref[jnp.maximum(b - 1, 0), 4].astype(F32)
        segs[0] = segs[0] + jnp.where(b > 0, before, 0.0)
        for j in range(2):
            a, c = segs[2 * j], segs[2 * j + 1]
            at = pl.ds(pl.multiple_of(b * span + j * OUT, 8), OUT)
            frames[0, at, :] = jnp.where(top, a, pltpu.roll(c, TAPS, 0))
            frames[1, at, :] = jnp.where(top, pltpu.roll(a, TAPS, 0), c)
        return 0

    lax.fori_loop(0, blocks, gather, 0)

    def turn(t, _):
        at = pl.ds(pl.multiple_of(t * 128, 128), 128)
        a, c = frames[0, at, :].T, frames[1, at, :].T
        both = jnp.stack([a, c], axis=1).astype(BF16)
        for ro in range(2):
            for p in range(POL):
                for g in range(GROUPS):
                    for jj in range(8):
                        out_ref[ro, 4 * jj + g, p, :, at] = both[ro * 64 + p * 32 + g * 8 + jj]
        return 0

    lax.fori_loop(0, blocks * span // 128, turn, 0)


def finish_call(x):
    blocks = x.shape[0]
    total = blocks * 4 * TAPS
    vmem = pl.BlockSpec(memory_space=pltpu.VMEM)
    return pl.pallas_call(
        finish_kernel,
        out_shape=jax.ShapeDtypeStruct((2, 32, POL, 2, total), BF16),
        in_specs=[vmem],
        out_specs=vmem,
        scratch_shapes=[pltpu.VMEM((2, total, 128), F32)],
        compiler_params=pltpu.CompilerParams(vmem_limit_bytes=32 * 1024 * 1024),
        name="finish",
    )(x)


def shards(voltages, delay_table, delay_index, delay_fraction, station_subarray):
    nz, ny = lax.axis_size("z"), lax.axis_size("y")
    rows = jnp.asarray(filter_rows())
    dft = jnp.asarray(dft_rows()).astype(BF16)
    found = fused_call(voltages, rows, dft, delay_table.reshape(-1, 128), delay_index, delay_fraction,
                       station_subarray.reshape(1, -1), nz, ny)
    return finish_call(found)


def solution(mesh):
    torus = Mesh(mesh.devices.reshape(8, 4, 2, 2, mesh.shape["stn"]), CHAN + ("stn",))
    placed = (P(None, CHAN, None, None, "stn"), P(), P(None, "stn"), P(None, "stn"), P("stn"))
    return jax.shard_map(
        shards,
        mesh=torus,
        in_specs=placed,
        out_specs=P(None, "stn", None, CHAN, None),
        check_vma=False,
    )
```
